256 devices in a mesh: front: 64 (over z, y, core), sect: 4 (over x).
Axes of the slice: x: 4, y: 4, z: 8, core: 2. Of those that a mesh axis runs over, the one named last changes fastest.
Arguments:
- pivot_rows: float32 [64, 4, 512, 512], P('front', 'sect'), may hold values from -6 to 6
- sections: float32 [64, 4, 4, 256, 512], P('front', 'sect'), may hold values from -6 to 6
- sect_vectors: bfloat16 [64, 4, 4, 256, 512], P('front', 'sect'), may hold values from -0.375 to 0.375
- sect_factors: bfloat16 [64, 4, 4, 512, 512], P('front', 'sect'), may hold values from -0.125 to 0.125
- routes: int32 [64, 4, 1024, 1], P('front', 'sect'), may hold values from 0 to 63; in each aligned block of 1024 rows (0 to 1023, 1024 to 2047, ..., all dimensions but the last counted through in order) at most 24 rows name the same one
- parent_vectors: bfloat16 [64, 4, 1536, 512], P('front', 'sect'), may hold values from -0.078125 to 0.078125
- parent_factor: bfloat16 [64, 512, 512], P('front'), may hold values from -0.25 to 0.25
Outputs:
- top_rows: float32 [64, 4, 512, 512], P('front', 'sect')
- parent_rows: float32 [64, 4, 1536, 512], P('front', 'sect')
The draws below stay inside these ranges and needn't reach their ends.
Inputs may be any that keep to these rules, and one draw needn't show every extreme that they name: `routes`: the rows of one section name each parent owner at most 24 times, a bound that some block reaches.
All inputs are finite; a program needn't handle non-finite values.
Results may differ from the reference program's by a relative error of at most 0.0003.
Values sent between devices are 32-bit elements; how exact they have to be, the bound alone decides.
No kernel may reach another device: no remote copies, remote signals or barrier semaphores. Data moves between devices by JAX's collectives and lax.ppermute only.
A program may use at most 128 MiB of HBM per device.

```python
import math
import jax
import jax.numpy as jnp
import numpy as np
from jax import lax

NRHS = 512
PW = 512
SEC = 256
PANELS = 4
FRONTS = 64
ROWS_DEV = 1024
CAPS = 24
PROWS = 1536
N_FRONT = 64
N_SECT = 4


def shard_levels(key, dims, split, smallest, high):
    def one(position, shards_of):
        draws = jax.random.uniform(jax.random.fold_in(jax.random.fold_in(key, 6), position), (shards_of,), jnp.float32, smallest / len(split), high / len(split))
        return jnp.repeat(jnp.exp(draws), dims[position] // shards_of).reshape((-1,) + (1,) * (len(dims) - position - 1))

    loudness = one(*split[0])
    for cut in split[1:]:
        loudness = loudness * one(*cut)
    return loudness


def routed_block(own_key, own, number, rows, number_of, top, limit, skew):
    sequence = jax.random.permutation(own_key, number_of)
    packed, ordinary = shares(number_of, rows * top, limit, skew, True), shares(number_of, rows * top, limit, skew, False)
    places = jnp.arange(number_of)

    def named(lengths, offset_by):
        used = int((lengths > 0).sum())
        fixed = max(1, used // 4)
        shifted = fixed + (places - fixed + offset_by * (used - fixed)) % max(1, number_of - fixed)
        return jnp.zeros((number_of,), jnp.int32).at[sequence[jnp.where(places < fixed, places, shifted)]].set(jnp.asarray(lengths, jnp.int32))

    lengths = jnp.where(number % 4 == 0, named(packed, number // 4), named(ordinary, number - number // 4 - 1))
    mixed = jax.random.permutation(jax.random.fold_in(own, 3), number_of)
    source_of, receiver = mixed[0:number_of // 2 * 2:2], mixed[1:number_of // 2 * 2:2]
    slack = jnp.minimum(lengths[source_of] - 1, limit - lengths[receiver]) // 2
    slack = jnp.where((source_of == sequence[0]) | (receiver == sequence[0]) | (lengths[receiver] == 0), 0, jnp.maximum(slack, 0))
    shifted = jax.random.randint(jax.random.fold_in(own, 4), (number_of // 2,), 0, 1 << 20) % (slack + 1)
    lengths = lengths.at[source_of].add(-shifted).at[receiver].add(shifted)
    members = jnp.searchsorted(jnp.cumsum(lengths), jnp.arange(rows * top), side="right").astype(jnp.int32)
    table = members.reshape(top, rows).T
    table = table[jax.random.permutation(jax.random.fold_in(own, 1), rows)]
    offset_by = jax.random.randint(jax.random.fold_in(own, 2), (rows, 1), 0, top)
    return jnp.take_along_axis(table, (jnp.arange(top)[None, :] + offset_by) % top, axis=1)


def shares(number_of, total, most, lean, full):
    weights = [(1 << 20) // math.isqrt(grade ** lean) + 1 for grade in range(1, number_of + 1)]
    largest = most if full else min(most, max(-(-total // number_of), total * weights[0] // sum(weights)))
    least = 1 if total - largest >= number_of - 1 else 0
    given, rest = [largest] + [least] * (number_of - 1), total - largest - least * (number_of - 1)
    while rest > 0:
        candidates = [i for i in range(1, number_of) if given[i] < largest] or [i for i in range(1, number_of) if given[i] < most]
        mass, remaining = sum([weights[i] for i in candidates]), rest
        for i in candidates:
            more = min(most - given[i], max(1, remaining * weights[i] // mass), rest)
            given[i] = given[i] + more
            rest = rest - more
    return np.array(given)


def bell_draw(own_key, dims, scale, reach, split=(), kind=jnp.bfloat16):
    values = jax.random.normal(own_key, dims, jnp.float32) * scale
    if len(split) > 0:
        values = shard_levels(own_key, dims, split, -0.22, 0.18) * values
    return jnp.clip(values, min=-reach, max=reach).astype(kind)


def setup_inputs(seed: int = 0) -> dict:
    splits = jax.random.split(jax.random.key(seed), 8)
    pivot_rows = bell_draw(splits[0], (FRONTS, PANELS, PW, NRHS), 1.0, 6.0, ((0, 64), (1, 4)), jnp.float32)
    sections = bell_draw(splits[1], (FRONTS, N_SECT, PANELS, SEC, NRHS), 1.0, 6.0, ((0, 64), (1, 4)), jnp.float32)
    sect_vectors = bell_draw(splits[2], (FRONTS, N_SECT, PANELS, SEC, PW), SEC ** -0.5, 0.375, ((0, 64), (1, 4)))
    sect_factors = bell_draw(splits[3], (FRONTS, N_SECT, PANELS, PW, PW), (4 * PW) ** -0.5, 0.125, ((0, 64), (1, 4)))
    routes_keys = jax.random.split(jax.random.fold_in(splits[4], 1), FRONTS * N_SECT * ROWS_DEV // ROWS_DEV)
    routes_turns = jax.random.permutation(jax.random.fold_in(splits[4], 3), FRONTS * N_SECT * ROWS_DEV // ROWS_DEV)
    routes = jax.vmap(lambda own, number: routed_block(jax.random.fold_in(splits[4], 2), own, number, ROWS_DEV, N_FRONT, 1, CAPS, 2))(routes_keys, routes_turns).reshape((FRONTS, N_SECT, ROWS_DEV, 1))
    parent_vectors = bell_draw(splits[5], (FRONTS, N_SECT, PROWS, PW), (N_SECT * PROWS) ** -0.5, 0.078125, ((0, 64), (1, 4)))
    parent_factor = bell_draw(splits[6], (FRONTS, PW, PW), PW ** -0.5, 0.25, ((0, 64),))
    return {"pivot_rows": pivot_rows, "sections": sections, "sect_vectors": sect_vectors, "sect_factors": sect_factors, "routes": routes, "parent_vectors": parent_vectors, "parent_factor": parent_factor}


highest = lax.Precision.HIGHEST


def reflect(pivot_block, row_block, vectors, factor):
    vectors = vectors.astype(jnp.float32)
    factor = factor.astype(jnp.float32)
    inner_sum = pivot_block + jnp.einsum('rp,rn->pn', vectors, row_block, precision=highest)
    change = jnp.einsum('qp,qn->pn', factor, inner_sum, precision=highest)
    return pivot_block - change, row_block - jnp.dot(vectors, change, precision=highest)


def front_chain(carried):
    pivots, blocks, vectors, factors = carried
    finished = []
    for panel_id in range(PANELS):
        pivot_block = pivots[panel_id]
        for step_id in range(N_SECT):
            owner_id = (panel_id + step_id) % N_SECT
            pivot_block, updated = reflect(pivot_block, blocks[owner_id, panel_id], vectors[owner_id, panel_id], factors[owner_id, panel_id])
            blocks = blocks.at[owner_id, panel_id].set(updated)
        finished.append(pivot_block)
    return jnp.stack(finished), blocks


def reference(pivot_rows, sections, sect_vectors, sect_factors, routes, parent_vectors, parent_factor):
    top_rows, updated = lax.map(front_chain, (pivot_rows, sections, sect_vectors, sect_factors))
    assembled = []
    projection = jnp.zeros((FRONTS, PW, NRHS), jnp.float32)
    for owner_id in range(N_SECT):
        contrib = updated[:, owner_id].reshape(FRONTS, ROWS_DEV, NRHS)
        destination = routes[:, owner_id, :, 0].astype(jnp.int32)
        onehot = (destination[:, :, None] == jnp.arange(FRONTS, dtype=jnp.int32)[None, None, :]).astype(jnp.int32)
        rank_slot = jnp.sum(jnp.cumsum(onehot, axis=1) * onehot, axis=2) - 1
        column_slot = (jnp.arange(FRONTS, dtype=jnp.int32)[:, None] * CAPS + rank_slot).astype(jnp.int32)
        parent = jnp.zeros((FRONTS, PROWS, NRHS), jnp.float32).at[destination, column_slot].set(contrib)
        assembled.append(parent)
        vectors = parent_vectors[:, owner_id].astype(jnp.float32)
        projection = projection + jnp.einsum('frp,frn->fpn', vectors, parent, precision=highest)
    change = jnp.einsum('fqp,fqn->fpn', parent_factor.astype(jnp.float32), projection, precision=highest)
    results = []
    for owner_id in range(N_SECT):
        vectors = parent_vectors[:, owner_id].astype(jnp.float32)
        results.append(assembled[owner_id] - jnp.einsum('frp,fpn->frn', vectors, change, precision=highest))
    return top_rows, jnp.stack(results, axis=1)
```

```python
import functools

import jax
import jax.numpy as jnp
from jax import lax
from jax.experimental import pallas as pl
from jax.experimental.pallas import tpu as pltpu
from jax.sharding import PartitionSpec as P

WIDTHS = (256, 256)
MIB = 1 << 20


def passed_along(value, steps):
    count = lax.axis_size("sect")
    pairs = [(source, (source + steps) % count) for source in range(count)]
    return lax.ppermute(value, "sect", pairs)


def halves(value):
    high = value.astype(jnp.bfloat16)
    low = (value - high.astype(jnp.float32)).astype(jnp.bfloat16)
    return high, low


def product(left, right, axis):
    dims = (((axis,), (0,)), ((), ()))
    high, low = halves(right)
    dot = functools.partial(
        lax.dot_general, dimension_numbers=dims, preferred_element_type=jnp.float32
    )
    return dot(left, low) + dot(left, high)


def reflect_kernel(panel, pivot, block, vectors, factor, pivot_out, block_out):
    change = product(factor[0], pivot[...] + product(vectors[0], block[0], 0), 0)
    pivot_out[...] = pivot[...] - change
    block_out[...] = block[0] - product(vectors[0], change, 1)


def reflect(panel, pivot, first, sections, vectors, factors, column, width):
    rows, size = vectors.shape[1:]
    pivot_spec = pl.BlockSpec((size, width), (lambda i, p: (0, column)) if first else (lambda i, p: (0, 0)))
    return pl.pallas_call(
        reflect_kernel,
        grid_spec=pltpu.PrefetchScalarGridSpec(
            num_scalar_prefetch=1,
            grid=(1,),
            in_specs=[
                pivot_spec,
                pl.BlockSpec((1, rows, width), lambda i, p: (p[0], 0, column)),
                pl.BlockSpec((1, rows, size), lambda i, p: (p[0], 0, 0)),
                pl.BlockSpec((1, size, size), lambda i, p: (p[0], 0, 0)),
            ],
            out_specs=[
                pl.BlockSpec((size, width), lambda i, p: (0, 0)),
                pl.BlockSpec((rows, width), lambda i, p: (0, 0)),
            ],
        ),
        out_shape=[
            jax.ShapeDtypeStruct((size, width), jnp.float32),
            jax.ShapeDtypeStruct((rows, width), jnp.float32),
        ],
        cost_estimate=pl.CostEstimate(
            flops=4 * width * size * (2 * rows + size),
            bytes_accessed=4 * width * 2 * (size + rows) + 2 * size * (rows + size),
            transcendentals=0,
        ),
        compiler_params=pltpu.CompilerParams(vmem_limit_bytes=20 * MIB),
        name="reflect",
    )(panel, pivot, sections, vectors, factors)


def pack_kernel(bases, slots, *refs):
    blocks, out = refs[:-1], refs[-1]
    out[...] = jnp.zeros_like(out)
    for step, block in enumerate(blocks):
        base = bases[step]

        @pl.loop(0, block.shape[0] // 16)
        def _(group, block=block, base=base):
            for inner in range(16):
                row = group * 16 + inner
                out[pl.ds(slots[base + row], 1), :] = block[pl.ds(row, 1), :]


def pack(bases, slots, blocks, total):
    width = blocks[0].shape[1]
    return pl.pallas_call(
        pack_kernel,
        grid_spec=pltpu.PrefetchScalarGridSpec(
            num_scalar_prefetch=2,
            grid=(1,),
            in_specs=[pl.BlockSpec(b.shape, lambda i, *_: (0, 0)) for b in blocks],
            out_specs=pl.BlockSpec((total, width), lambda i, *_: (0, 0)),
        ),
        out_shape=jax.ShapeDtypeStruct((total, width), jnp.float32),
        cost_estimate=pl.CostEstimate(
            flops=total * width, bytes_accessed=4 * width * 5 * total // 3, transcendentals=0
        ),
        compiler_params=pltpu.CompilerParams(vmem_limit_bytes=20 * MIB),
        name="pack",
    )(bases, slots, *blocks)


def project_kernel(owner, vectors, rows, *outs):
    scratch = outs[-1]
    scratch[...] = product(vectors[...], rows[...], 0)
    count = len(outs) - 1
    part = scratch.shape[0] // count
    for away in range(count):
        start = pl.multiple_of(lax.rem(owner[0] + away, count) * part, part)
        outs[away][...] = scratch[pl.ds(start, part), :]


def project(owner, vectors, rows, count):
    total, width = rows.shape
    size = vectors.shape[1]
    part = size // count
    return pl.pallas_call(
        project_kernel,
        grid_spec=pltpu.PrefetchScalarGridSpec(
            num_scalar_prefetch=1,
            grid=(1,),
            in_specs=[
                pl.BlockSpec((total, size), lambda i, p: (0, 0)),
                pl.BlockSpec((total, width), lambda i, p: (0, 0)),
            ],
            out_specs=[pl.BlockSpec((part, width), lambda i, p: (0, 0))] * count,
            scratch_shapes=[pltpu.VMEM((size, width), jnp.float32)],
        ),
        out_shape=[jax.ShapeDtypeStruct((part, width), jnp.float32)] * count,
        cost_estimate=pl.CostEstimate(
            flops=4 * total * size * width,
            bytes_accessed=4 * width * (total + size) + 2 * total * size,
            transcendentals=0,
        ),
        compiler_params=pltpu.CompilerParams(vmem_limit_bytes=24 * MIB),
        name="project",
    )(owner, vectors, rows)


def finish_kernel(refs_parts, owner, factor, vectors, rows, *refs):
    out, scratch = refs[-2:]
    count = refs_parts
    parts = refs[:count]
    part = scratch.shape[0] // count

    @pl.when(pl.program_id(0) == 0)
    def _():
        for away in range(count):
            start = pl.multiple_of(lax.rem(owner[0] + count - away, count) * part, part)
            scratch[pl.ds(start, part), :] = parts[away][...]
        scratch[...] = product(factor[...], scratch[...], 0)

    out[...] = rows[...] - product(vectors[...], scratch[...], 1)


def finish(owner, factor, vectors, rows, parts, whole, column, columns):
    total, width = rows.shape
    size = vectors.shape[1]
    tile = total // 4
    kept = [] if whole is None else [whole]
    return pl.pallas_call(
        functools.partial(finish_kernel, len(parts)),
        grid_spec=pltpu.PrefetchScalarGridSpec(
            num_scalar_prefetch=1,
            grid=(total // tile,),
            in_specs=[
                pl.BlockSpec((size, size), lambda i, p: (0, 0)),
                pl.BlockSpec((tile, size), lambda i, p: (i, 0)),
                pl.BlockSpec((tile, width), lambda i, p: (i, 0)),
                *[pl.BlockSpec(q.shape, lambda i, p: (0, 0)) for q in parts],
                *[pl.BlockSpec(memory_space=pl.ANY) for _ in kept],
            ],
            out_specs=pl.BlockSpec((tile, width), lambda i, p: (i, column)),
            scratch_shapes=[pltpu.VMEM((size, width), jnp.float32)],
        ),
        out_shape=jax.ShapeDtypeStruct((total, columns), jnp.float32),
        input_output_aliases={4 + len(parts): 0} if kept else {},
        cost_estimate=pl.CostEstimate(
            flops=4 * size * width * (total + size),
            bytes_accessed=4 * width * (2 * total + size) + 2 * size * (total + size),
            transcendentals=0,
        ),
        compiler_params=pltpu.CompilerParams(vmem_limit_bytes=24 * MIB),
        name="finish",
    )(owner, factor, vectors, rows, *parts, *kept)


def slots_of(destination, owners, capacity):
    onehot = destination[:, None] == jnp.arange(owners, dtype=jnp.int32)[None, :]
    onehot = onehot.astype(jnp.float32).reshape(-1, 128, owners)
    lower = jnp.tril(jnp.ones((128, 128), jnp.float32), -1)
    within = jnp.einsum("rs,bso->bro", lower, onehot)
    sums = jnp.sum(onehot, axis=1)
    ahead = jnp.cumsum(sums, axis=0) - sums
    rank = jnp.sum((within + ahead[:, None, :]) * onehot, axis=2)
    return destination * capacity + rank.reshape(-1).astype(jnp.int32)


def local(pivot_rows, sections, sect_vectors, sect_factors, routes, parent_vectors, parent_factor):
    me = lax.axis_index("sect")
    count = lax.axis_size("sect")
    owners = lax.axis_size("front")
    sections, sect_vectors, sect_factors = sections[0, 0], sect_vectors[0, 0], sect_factors[0, 0]
    panels, rows = sections.shape[:2]
    capacity = 3 * panels * rows // (2 * owners)
    total = owners * capacity
    slots = slots_of(routes[0, 0, :, 0], owners, capacity)
    panel_at = [((me - step) % count).astype(jnp.int32)[None] for step in range(count)]
    bases = jnp.concatenate(panel_at) * rows
    owner = me.astype(jnp.int32)[None]
    vectors, factor = parent_vectors[0, 0], parent_factor[0]
    tops, out = [], None
    start = 0
    for width in WIDTHS:
        column, start = start // width, start + width
        pivot, blocks = pivot_rows[0, 0], []
        for step in range(count):
            pivot, block = reflect(
                panel_at[step], pivot, step == 0, sections, sect_vectors, sect_factors, column, width
            )
            blocks.append(block)
            pivot = passed_along(pivot, 1)
        tops.append(pivot)
        packed = pack(bases, slots, blocks, total).reshape(owners, capacity, width)
        arrived = lax.all_to_all(packed, "front", split_axis=0, concat_axis=0, tiled=True)
        arrived = arrived.reshape(total, width)
        own, *others = project(owner, vectors, arrived, count)
        for away, part in enumerate(others):
            own = own + passed_along(part, away + 1)
        parts = [own] + [passed_along(own, away) for away in range(1, count)]
        out = finish(owner, factor, vectors, arrived, parts, out, column, sections.shape[-1])
    return (jnp.concatenate(tops, axis=1)[None, None], out[None, None])


def solution(mesh):
    in_specs = (
        P("front", "sect", None, None),
        P("front", "sect", None, None, None),
        P("front", "sect", None, None, None),
        P("front", "sect", None, None, None),
        P("front", "sect", None, None),
        P("front", "sect", None, None),
        P("front", None, None),
    )
    out_specs = (P("front", "sect", None, None), P("front", "sect", None, None))
    return jax.shard_map(local, mesh=mesh, in_specs=in_specs, out_specs=out_specs, check_vma=False)
```

```python
import functools

import jax
import jax.numpy as jnp
from jax import lax
from jax.experimental import pallas as pl
from jax.experimental.pallas import tpu as pltpu
from jax.sharding import PartitionSpec as P


CHUNKS = (((0, 128), (128, 128)), ((256, 128), (384, 128)))
MIB = 1 << 20


def passed_along(value, steps):
    count = lax.axis_size("sect")
    pairs = [(source, (source + steps) % count) for source in range(count)]
    return lax.ppermute(value, "sect", pairs)


def halves(value):
    high = value.astype(jnp.bfloat16)
    low = (value - high.astype(jnp.float32)).astype(jnp.bfloat16)
    return high, low


def product(left, right, axis):
    width = right.shape[1]
    dot = functools.partial(
        lax.dot_general,
        dimension_numbers=(((axis,), (0,)), ((), ())),
        preferred_element_type=jnp.float32,
    )
    high, low = halves(right)
    if width < 256:
        both = dot(left, jnp.concatenate([low, high], axis=1))
        return both[:, :width] + both[:, width:]
    return dot(left, low) + dot(left, high)


def first_kernel(panel, pivot, block, vectors, factor, pivot_out, block_out):
    change = product(factor[0], pivot[...] + product(vectors[0], block[0], 0), 0)
    pivot_out[...] = pivot[...] - change
    block_out[...] = block[0] - product(vectors[0], change, 1)


def reflect_kernel(step, panel, pivot, block, vectors, turned, factor, pivot_out, block_out):
    change = product(factor[step], pivot[...] + product(turned[step], block[0], 1), 1)
    pivot_out[...] = pivot[...] - change
    block_out[...] = block[0] - product(vectors[step], change, 1)


def place_rows(slots, base, blocks, out):
    @pl.loop(0, blocks[0].shape[0] // 16)
    def _(group):
        for inner in range(16):
            row = group * 16 + inner
            pieces = [block[pl.ds(row, 1), :] for block in blocks]
            value = jnp.concatenate(pieces, axis=1) if len(pieces) > 1 else pieces[0]
            out[pl.ds(slots[base + row], 1), :] = value


def last_kernel(step, panel, slots, pivot, block, vectors, turned, factor, packed, *refs):
    *others, pivot_out, packed_out, updated = refs
    packed_out[...] = packed[...]
    reflect_kernel(step, panel, pivot, block, vectors, turned, factor, pivot_out, updated)
    place_rows(slots, panel[0] * updated.shape[0], [*others, updated], packed_out)


def reflect(panel, step, pivot, column, width, sections, weights):
    rows = sections.shape[1]
    size = pivot.shape[0]
    at = column // width
    if len(weights) == 2:
        body = first_kernel
        weight_specs = [
            pl.BlockSpec((1, rows, size), lambda i, p: (p[0], 0, 0)),
            pl.BlockSpec((1, size, size), lambda i, p: (p[0], 0, 0)),
        ]
    else:
        body = functools.partial(reflect_kernel, step)
        weight_specs = [pl.BlockSpec(memory_space=pltpu.VMEM)] * 3
    pivot_at = at if step == 0 else 0
    return pl.pallas_call(
        body,
        grid_spec=pltpu.PrefetchScalarGridSpec(
            num_scalar_prefetch=1,
            grid=(1,),
            in_specs=[
                pl.BlockSpec((size, width), lambda i, p: (0, pivot_at)),
                pl.BlockSpec((1, rows, width), lambda i, p: (p[0], 0, at)),
                *weight_specs,
            ],
            out_specs=[
                pl.BlockSpec((size, width), lambda i, p: (0, 0)),
                pl.BlockSpec((rows, width), lambda i, p: (0, 0)),
            ],
        ),
        out_shape=[
            jax.ShapeDtypeStruct((size, width), jnp.float32),
            jax.ShapeDtypeStruct((rows, width), jnp.float32),
        ],
        cost_estimate=pl.CostEstimate(
            flops=4 * width * size * (2 * rows + size),
            bytes_accessed=4 * width * 2 * (size + rows) + 2 * size * (rows + size),
            transcendentals=0,
        ),
        compiler_params=pltpu.CompilerParams(vmem_limit_bytes=16 * MIB),
        name="reflect",
    )(panel, pivot, sections, *weights)


def reflect_last(panel, step, slots, pivot, column, sections, weights, packed, others):
    rows = sections.shape[1]
    size, width = pivot.shape
    total, wide = packed.shape
    at = column // width
    return pl.pallas_call(
        functools.partial(last_kernel, step),
        grid_spec=pltpu.PrefetchScalarGridSpec(
            num_scalar_prefetch=2,
            grid=(1,),
            in_specs=[
                pl.BlockSpec((size, width), lambda i, p, s: (0, 0)),
                pl.BlockSpec((1, rows, width), lambda i, p, s: (p[0], 0, at)),
                *[pl.BlockSpec(memory_space=pltpu.VMEM)] * 3,
                pl.BlockSpec((total, wide), lambda i, p, s: (0, 0)),
                *[pl.BlockSpec(other.shape, lambda i, p, s: (0, 0)) for other in others],
            ],
            out_specs=[
                pl.BlockSpec((size, width), lambda i, p, s: (0, 0)),
                pl.BlockSpec((total, wide), lambda i, p, s: (0, 0)),
            ],
            scratch_shapes=[pltpu.VMEM((rows, width), jnp.float32)],
        ),
        out_shape=[
            pltpu.HBM((size, width), jnp.float32),
            pltpu.HBM((total, wide), jnp.float32),
        ],
        cost_estimate=pl.CostEstimate(
            flops=4 * width * size * (2 * rows + size),
            bytes_accessed=8 * width * (size + rows) + 8 * wide * total + 2 * size * (rows + size),
            transcendentals=0,
        ),
        compiler_params=pltpu.CompilerParams(vmem_limit_bytes=16 * MIB),
        name="reflect_last",
    )(panel, slots, pivot, sections, *weights, packed, *others)


def stage_kernel(panels, vectors, factor, vectors_out, turned_out, factor_out):
    step = pl.program_id(0)
    vectors_out[step] = vectors[0]
    turned_out[step] = vectors[0].T
    factor_out[step] = factor[0].T


def stage(panels, vectors, factors):
    count, rows, size = vectors.shape
    whole = pl.BlockSpec(memory_space=pltpu.VMEM)
    return pl.pallas_call(
        stage_kernel,
        grid_spec=pltpu.PrefetchScalarGridSpec(
            num_scalar_prefetch=1,
            grid=(count,),
            in_specs=[
                pl.BlockSpec((1, rows, size), lambda i, p: (p[i], 0, 0)),
                pl.BlockSpec((1, size, size), lambda i, p: (p[i], 0, 0)),
            ],
            out_specs=[whole, whole, whole],
        ),
        out_shape=[
            pltpu.VMEM((count, rows, size), vectors.dtype),
            pltpu.VMEM((count, size, rows), vectors.dtype),
            pltpu.VMEM((count, size, size), vectors.dtype),
        ],
        cost_estimate=pl.CostEstimate(
            flops=0, bytes_accessed=2 * count * size * (rows + size), transcendentals=0
        ),
        compiler_params=pltpu.CompilerParams(vmem_limit_bytes=16 * MIB),
        name="stage",
    )(panels, vectors, factors)


def pack_kernel(steps, bases, slots, *refs):
    blocks, out = refs[:-1], refs[-1]
    out[...] = jnp.zeros_like(out)
    for step in range(steps):
        place_rows(slots, bases[step], blocks[step::steps], out)


def pack(bases, slots, streams, total):
    blocks = [block for stream in streams for block in stream]
    wide = sum(stream[0].shape[1] for stream in streams)
    return pl.pallas_call(
        functools.partial(pack_kernel, len(streams[0])),
        grid_spec=pltpu.PrefetchScalarGridSpec(
            num_scalar_prefetch=2,
            grid=(1,),
            in_specs=[pl.BlockSpec(b.shape, lambda i, *_: (0, 0)) for b in blocks],
            out_specs=pl.BlockSpec((total, wide), lambda i, *_: (0, 0)),
        ),
        out_shape=jax.ShapeDtypeStruct((total, wide), jnp.float32),
        cost_estimate=pl.CostEstimate(
            flops=total * wide, bytes_accessed=6 * wide * total, transcendentals=0
        ),
        compiler_params=pltpu.CompilerParams(vmem_limit_bytes=16 * MIB),
        name="pack",
    )(bases, slots, *blocks)


def project_kernel(owner, vectors, rows, *outs):
    scratch = outs[-1]
    scratch[...] = product(vectors[...], rows[...], 0)
    count = len(outs) - 1
    part = scratch.shape[0] // count
    for away in range(count):
        start = pl.multiple_of(lax.rem(owner[0] + away, count) * part, part)
        outs[away][...] = scratch[pl.ds(start, part), :]


def project(owner, vectors, rows, count):
    total, width = rows.shape
    size = vectors.shape[1]
    part = size // count
    return pl.pallas_call(
        project_kernel,
        grid_spec=pltpu.PrefetchScalarGridSpec(
            num_scalar_prefetch=1,
            grid=(1,),
            in_specs=[
                pl.BlockSpec((total, size), lambda i, p: (0, 0)),
                pl.BlockSpec((total, width), lambda i, p: (0, 0)),
            ],
            out_specs=[pl.BlockSpec((part, width), lambda i, p: (0, 0))] * count,
            scratch_shapes=[pltpu.VMEM((size, width), jnp.float32)],
        ),
        out_shape=[jax.ShapeDtypeStruct((part, width), jnp.float32)] * count,
        cost_estimate=pl.CostEstimate(
            flops=4 * total * size * width,
            bytes_accessed=4 * width * (total + size) + 2 * total * size,
            transcendentals=0,
        ),
        compiler_params=pltpu.CompilerParams(vmem_limit_bytes=16 * MIB),
        name="project",
    )(owner, vectors, rows)


def finish_kernel(refs_parts, owner, factor, vectors, rows, *refs):
    out, scratch = refs[-2:]
    count = refs_parts
    parts = refs[:count]
    part = scratch.shape[0] // count

    @pl.when(pl.program_id(0) == 0)
    def _():
        for away in range(count):
            start = pl.multiple_of(lax.rem(owner[0] + count - away, count) * part, part)
            scratch[pl.ds(start, part), :] = parts[away][...]
        scratch[...] = product(factor[...], scratch[...], 0)

    out[...] = rows[...] - product(vectors[...], scratch[...], 1)


def finish(owner, factor, vectors, rows, parts, whole, column, columns):
    total, width = rows.shape
    size = vectors.shape[1]
    tile = total // 4
    kept = [] if whole is None else [whole]
    return pl.pallas_call(
        functools.partial(finish_kernel, len(parts)),
        grid_spec=pltpu.PrefetchScalarGridSpec(
            num_scalar_prefetch=1,
            grid=(total // tile,),
            in_specs=[
                pl.BlockSpec((size, size), lambda i, p: (0, 0)),
                pl.BlockSpec((tile, size), lambda i, p: (i, 0)),
                pl.BlockSpec((tile, width), lambda i, p: (i, 0)),
                *[pl.BlockSpec(q.shape, lambda i, p: (0, 0)) for q in parts],
                *[pl.BlockSpec(memory_space=pl.ANY) for _ in kept],
            ],
            out_specs=pl.BlockSpec((tile, width), lambda i, p: (i, column)),
            scratch_shapes=[pltpu.VMEM((size, width), jnp.float32)],
        ),
        out_shape=jax.ShapeDtypeStruct((total, columns), jnp.float32),
        input_output_aliases={4 + len(parts): 0} if kept else {},
        cost_estimate=pl.CostEstimate(
            flops=4 * size * width * (total + size),
            bytes_accessed=4 * width * (2 * total + size) + 2 * size * (total + size),
            transcendentals=0,
        ),
        compiler_params=pltpu.CompilerParams(vmem_limit_bytes=16 * MIB),
        name="finish",
    )(owner, factor, vectors, rows, *parts, *kept)


def join_kernel(columns, *refs):
    for column, ref in zip(columns, refs[:-1]):
        refs[-1][:, column : column + ref.shape[1]] = ref[...]


def join(columns, pieces):
    size, total = pieces[0].shape[0], sum(piece.shape[1] for piece in pieces)
    tile = size // 2
    return pl.pallas_call(
        functools.partial(join_kernel, columns),
        grid=(2,),
        in_specs=[pl.BlockSpec((tile, piece.shape[1]), lambda i: (i, 0)) for piece in pieces],
        out_specs=pl.BlockSpec((tile, total), lambda i: (i, 0)),
        out_shape=jax.ShapeDtypeStruct((size, total), jnp.float32),
        cost_estimate=pl.CostEstimate(flops=0, bytes_accessed=8 * size * total, transcendentals=0),
        compiler_params=pltpu.CompilerParams(vmem_limit_bytes=16 * MIB),
        name="join",
    )(*pieces)


def slots_of(destination, owners, capacity):
    onehot = destination[:, None] == jnp.arange(owners, dtype=jnp.int32)[None, :]
    onehot = onehot.astype(jnp.float32).reshape(-1, 128, owners)
    lower = jnp.tril(jnp.ones((128, 128), jnp.float32), -1)
    within = jnp.einsum("rs,bso->bro", lower, onehot)
    sums = jnp.sum(onehot, axis=1)
    ahead = jnp.cumsum(sums, axis=0) - sums
    rank = jnp.sum((within + ahead[:, None, :]) * onehot, axis=2)
    return destination * capacity + rank.reshape(-1).astype(jnp.int32)


def local(pivot_rows, sections, sect_vectors, sect_factors, routes, parent_vectors, parent_factor):
    me = lax.axis_index("sect")
    count = lax.axis_size("sect")
    owners = lax.axis_size("front")
    pivots = in_hbm(pivot_rows[0, 0])
    sections, sect_vectors = in_hbm(sections[0, 0]), in_hbm(sect_vectors[0, 0])
    sect_factors = in_hbm(sect_factors[0, 0])
    panels, rows = sections.shape[:2]
    capacity = 3 * panels * rows // (2 * owners)
    total = owners * capacity
    panel_at = [((me - step) % count).astype(jnp.int32)[None] for step in range(count)]
    slots = slots_of(routes[0, 0, :, 0], owners, capacity)
    bases = jnp.concatenate(panel_at) * rows
    owner = me.astype(jnp.int32)[None]
    vectors, factor = parent_vectors[0, 0], parent_factor[0]
    weights = stage(jnp.concatenate(panel_at), sect_vectors, sect_factors)
    tops, out = [], None
    for chunk, streams in enumerate(CHUNKS):
        column, width = streams[0][0], sum(width for _, width in streams)
        updated, moving = [], []
        for first, narrow in streams:
            pivot, blocks = pivots, []
            for step in range(count - 1):
                direct = chunk == 0 and step == 0
                pivot, block = reflect(
                    panel_at[step], step, pivot, first, narrow, sections,
                    (sect_vectors, sect_factors) if direct else weights,
                )
                blocks.append(block)
                pivot = passed_along(pivot, 1)
            updated.append(blocks)
            moving.append(pivot)
        packed = pack(bases, slots, updated, total)
        others = []
        for stream, (first, narrow) in enumerate(streams):
            last = stream == len(streams) - 1
            if last:
                pivot, packed = reflect_last(
                    panel_at[-1], count - 1, slots, moving[stream], first, sections, weights,
                    packed, others,
                )
            else:
                pivot, block = reflect(
                    panel_at[-1], count - 1, moving[stream], first, narrow, sections, weights
                )
                others.append(block)
            tops.append(passed_along(pivot, 1))
        arrived = lax.all_to_all(
            packed.reshape(owners, capacity, width), "front", split_axis=0, concat_axis=0, tiled=True
        ).reshape(total, width)
        own, *others = project(owner, vectors, arrived, count)
        others = [passed_along(part, away + 1) for away, part in enumerate(others)]
        for part in others:
            own = own + part
        parts = [own] + [passed_along(own, away) for away in range(1, count)]
        out = finish(owner, factor, vectors, arrived, parts, out, column // width, sections.shape[-1])
    top = join([column for streams in CHUNKS for column, _ in streams], tops)
    return (top[None, None], out[None, None])


def in_hbm(value):
    return pltpu.with_memory_space_constraint(value, pltpu.HBM)


def solution(mesh):
    in_specs = (
        P("front", "sect", None, None),
        P("front", "sect", None, None, None),
        P("front", "sect", None, None, None),
        P("front", "sect", None, None, None),
        P("front", "sect", None, None),
        P("front", "sect", None, None),
        P("front", None, None),
    )
    out_specs = (P("front", "sect", None, None), P("front", "sect", None, None))
    return jax.shard_map(local, mesh=mesh, in_specs=in_specs, out_specs=out_specs, check_vma=False)
```

```python
import functools

import jax
import jax.numpy as jnp
from jax import lax
from jax.experimental import pallas as pl
from jax.experimental.pallas import tpu as pltpu
from jax.sharding import PartitionSpec as P


CHUNKS = (((0, 128), (128, 128)), ((256, 128), (384, 128)))
MIB = 1 << 20


def passed_along(value, steps):
    count = lax.axis_size("sect")
    pairs = [(source, (source + steps) % count) for source in range(count)]
    return lax.ppermute(value, "sect", pairs)


def halves(value):
    high = value.astype(jnp.bfloat16)
    low = (value - high.astype(jnp.float32)).astype(jnp.bfloat16)
    return high, low


def product(left, right, axis):
    width = right.shape[1]
    dot = functools.partial(
        lax.dot_general,
        dimension_numbers=(((axis,), (0,)), ((), ())),
        preferred_element_type=jnp.float32,
    )
    high, low = halves(right)
    if width < 256:
        both = dot(left, jnp.concatenate([low, high], axis=1))
        return both[:, :width] + both[:, width:]
    return dot(left, low) + dot(left, high)


def first_kernel(panel, pivot, block, vectors, factor, pivot_out, block_out):
    change = product(factor[0], pivot[...] + product(vectors[0], block[0], 0), 0)
    pivot_out[...] = pivot[...] - change
    block_out[...] = block[0] - product(vectors[0], change, 1)


def reflect_kernel(step, panel, pivot, block, vectors, turned, factor, pivot_out, block_out):
    at = step - 1
    change = product(factor[at], pivot[...] + product(turned[at], block[0], 1), 1)
    pivot_out[...] = pivot[...] - change
    block_out[...] = block[0] - product(vectors[at], change, 1)


def place_rows(slots, base, blocks, out):
    @pl.loop(0, blocks[0].shape[0] // 16)
    def _(group):
        for inner in range(16):
            row = group * 16 + inner
            pieces = [block[pl.ds(row, 1), :] for block in blocks]
            value = jnp.concatenate(pieces, axis=1) if len(pieces) > 1 else pieces[0]
            out[pl.ds(slots[base + row], 1), :] = value


def last_kernel(step, panel, slots, pivot, block, vectors, turned, factor, packed, *refs):
    *others, pivot_out, packed_out, updated = refs
    packed_out[...] = packed[...]
    reflect_kernel(step, panel, pivot, block, vectors, turned, factor, pivot_out, updated)
    place_rows(slots, panel[0] * updated.shape[0], [*others, updated], packed_out)


def reflect(panel, step, pivot, column, width, sections, weights):
    rows = sections.shape[1]
    size = pivot.shape[0]
    at = column // width
    if len(weights) == 2:
        body = first_kernel
        weight_specs = [
            pl.BlockSpec((1, rows, size), lambda i, p: (p[0], 0, 0)),
            pl.BlockSpec((1, size, size), lambda i, p: (p[0], 0, 0)),
        ]
    else:
        body = functools.partial(reflect_kernel, step)
        weight_specs = [pl.BlockSpec(memory_space=pltpu.VMEM)] * 3
    pivot_at = at if step == 0 else 0
    return pl.pallas_call(
        body,
        grid_spec=pltpu.PrefetchScalarGridSpec(
            num_scalar_prefetch=1,
            grid=(1,),
            in_specs=[
                pl.BlockSpec((size, width), lambda i, p: (0, pivot_at)),
                pl.BlockSpec((1, rows, width), lambda i, p: (p[0], 0, at)),
                *weight_specs,
            ],
            out_specs=[
                pl.BlockSpec((size, width), lambda i, p: (0, 0)),
                pl.BlockSpec((rows, width), lambda i, p: (0, 0)),
            ],
        ),
        out_shape=[
            jax.ShapeDtypeStruct((size, width), jnp.float32),
            pltpu.VMEM((rows, width), jnp.float32),
        ],
        cost_estimate=pl.CostEstimate(
            flops=4 * width * size * (2 * rows + size),
            bytes_accessed=4 * width * 2 * (size + rows) + 2 * size * (rows + size),
            transcendentals=0,
        ),
        compiler_params=pltpu.CompilerParams(vmem_limit_bytes=16 * MIB),
        name="reflect",
    )(panel, pivot, sections, *weights)


def reflect_last(panel, step, slots, pivot, column, sections, weights, packed, others):
    rows = sections.shape[1]
    size, width = pivot.shape
    total, wide = packed.shape
    at = column // width
    return pl.pallas_call(
        functools.partial(last_kernel, step),
        grid_spec=pltpu.PrefetchScalarGridSpec(
            num_scalar_prefetch=2,
            grid=(1,),
            in_specs=[
                pl.BlockSpec((size, width), lambda i, p, s: (0, 0)),
                pl.BlockSpec((1, rows, width), lambda i, p, s: (p[0], 0, at)),
                *[pl.BlockSpec(memory_space=pltpu.VMEM)] * 3,
                pl.BlockSpec(memory_space=pltpu.VMEM),
                *[pl.BlockSpec(other.shape, lambda i, p, s: (0, 0)) for other in others],
            ],
            out_specs=[
                pl.BlockSpec((size, width), lambda i, p, s: (0, 0)),
                pl.BlockSpec((total, wide), lambda i, p, s: (0, 0)),
            ],
            scratch_shapes=[pltpu.VMEM((rows, width), jnp.float32)],
        ),
        out_shape=[
            pltpu.HBM((size, width), jnp.float32),
            pltpu.HBM((total, wide), jnp.float32),
        ],
        cost_estimate=pl.CostEstimate(
            flops=4 * width * size * (2 * rows + size),
            bytes_accessed=8 * width * (size + rows) + 8 * wide * total + 2 * size * (rows + size),
            transcendentals=0,
        ),
        compiler_params=pltpu.CompilerParams(vmem_limit_bytes=16 * MIB),
        name="reflect_last",
    )(panel, slots, pivot, sections, *weights, packed, *others)


def stage_kernel(panels, vectors, factor, vectors_out, turned_out, factor_out):
    step = pl.program_id(0)
    vectors_out[step] = vectors[0]
    turned_out[step] = vectors[0].T
    factor_out[step] = factor[0].T


def stage(panels, vectors, factors):
    rows, size = vectors.shape[1:]
    count = panels.shape[0]
    whole = pl.BlockSpec(memory_space=pltpu.VMEM)
    return pl.pallas_call(
        stage_kernel,
        grid_spec=pltpu.PrefetchScalarGridSpec(
            num_scalar_prefetch=1,
            grid=(count,),
            in_specs=[
                pl.BlockSpec((1, rows, size), lambda i, p: (p[i], 0, 0)),
                pl.BlockSpec((1, size, size), lambda i, p: (p[i], 0, 0)),
            ],
            out_specs=[whole, whole, whole],
        ),
        out_shape=[
            pltpu.VMEM((count, rows, size), vectors.dtype),
            pltpu.VMEM((count, size, rows), vectors.dtype),
            pltpu.VMEM((count, size, size), vectors.dtype),
        ],
        cost_estimate=pl.CostEstimate(
            flops=0, bytes_accessed=2 * count * size * (rows + size), transcendentals=0
        ),
        compiler_params=pltpu.CompilerParams(vmem_limit_bytes=16 * MIB),
        name="stage",
    )(panels, vectors, factors)


def pack_kernel(steps, bases, slots, *refs):
    blocks, out = refs[:-1], refs[-1]
    out[...] = jnp.zeros_like(out)
    for step in range(steps):
        place_rows(slots, bases[step], blocks[step::steps], out)


def pack(bases, slots, streams, total):
    blocks = [block for stream in streams for block in stream]
    wide = sum(stream[0].shape[1] for stream in streams)
    return pl.pallas_call(
        functools.partial(pack_kernel, len(streams[0])),
        grid_spec=pltpu.PrefetchScalarGridSpec(
            num_scalar_prefetch=2,
            grid=(1,),
            in_specs=[pl.BlockSpec(b.shape, lambda i, *_: (0, 0)) for b in blocks],
            out_specs=pl.BlockSpec(memory_space=pltpu.VMEM),
        ),
        out_shape=pltpu.VMEM((total, wide), jnp.float32),
        cost_estimate=pl.CostEstimate(
            flops=total * wide, bytes_accessed=6 * wide * total, transcendentals=0
        ),
        compiler_params=pltpu.CompilerParams(vmem_limit_bytes=16 * MIB),
        name="pack",
    )(bases, slots, *blocks)


def project_kernel(owner, vectors, rows, *outs):
    scratch = outs[-1]
    scratch[...] = product(vectors[...], rows[...], 0)
    count = len(outs) - 1
    part = scratch.shape[0] // count
    for away in range(count):
        start = pl.multiple_of(lax.rem(owner[0] + away, count) * part, part)
        outs[away][...] = scratch[pl.ds(start, part), :]


def project(owner, vectors, rows, count):
    total, width = rows.shape
    size = vectors.shape[1]
    part = size // count
    return pl.pallas_call(
        project_kernel,
        grid_spec=pltpu.PrefetchScalarGridSpec(
            num_scalar_prefetch=1,
            grid=(1,),
            in_specs=[
                pl.BlockSpec((total, size), lambda i, p: (0, 0)),
                pl.BlockSpec((total, width), lambda i, p: (0, 0)),
            ],
            out_specs=[pl.BlockSpec((part, width), lambda i, p: (0, 0))] * count,
            scratch_shapes=[pltpu.VMEM((size, width), jnp.float32)],
        ),
        out_shape=[jax.ShapeDtypeStruct((part, width), jnp.float32)] * count,
        cost_estimate=pl.CostEstimate(
            flops=4 * total * size * width,
            bytes_accessed=4 * width * (total + size) + 2 * total * size,
            transcendentals=0,
        ),
        compiler_params=pltpu.CompilerParams(vmem_limit_bytes=16 * MIB),
        name="project",
    )(owner, vectors, rows)


def finish_kernel(refs_parts, owner, factor, vectors, rows, *refs):
    out, scratch = refs[-2:]
    count = refs_parts
    parts = refs[:count]
    part = scratch.shape[0] // count

    @pl.when(pl.program_id(0) == 0)
    def _():
        for away in range(count):
            start = pl.multiple_of(lax.rem(owner[0] + count - away, count) * part, part)
            scratch[pl.ds(start, part), :] = parts[away][...]
        scratch[...] = product(factor[...], scratch[...], 0)

    out[...] = rows[...] - product(vectors[...], scratch[...], 1)


def finish(owner, factor, vectors, rows, parts, whole, column, columns):
    total, width = rows.shape
    size = vectors.shape[1]
    tile = total // 4
    kept = [] if whole is None else [whole]
    return pl.pallas_call(
        functools.partial(finish_kernel, len(parts)),
        grid_spec=pltpu.PrefetchScalarGridSpec(
            num_scalar_prefetch=1,
            grid=(total // tile,),
            in_specs=[
                pl.BlockSpec((size, size), lambda i, p: (0, 0)),
                pl.BlockSpec((tile, size), lambda i, p: (i, 0)),
                pl.BlockSpec((tile, width), lambda i, p: (i, 0)),
                *[pl.BlockSpec(q.shape, lambda i, p: (0, 0)) for q in parts],
                *[pl.BlockSpec(memory_space=pl.ANY) for _ in kept],
            ],
            out_specs=pl.BlockSpec((tile, width), lambda i, p: (i, column)),
            scratch_shapes=[pltpu.VMEM((size, width), jnp.float32)],
        ),
        out_shape=jax.ShapeDtypeStruct((total, columns), jnp.float32),
        input_output_aliases={4 + len(parts): 0} if kept else {},
        cost_estimate=pl.CostEstimate(
            flops=4 * size * width * (total + size),
            bytes_accessed=4 * width * (2 * total + size) + 2 * size * (total + size),
            transcendentals=0,
        ),
        compiler_params=pltpu.CompilerParams(vmem_limit_bytes=16 * MIB),
        name="finish",
    )(owner, factor, vectors, rows, *parts, *kept)


def join_kernel(columns, *refs):
    for column, ref in zip(columns, refs[:-1]):
        refs[-1][:, column : column + ref.shape[1]] = ref[...]


def join(columns, pieces):
    size, total = pieces[0].shape[0], sum(piece.shape[1] for piece in pieces)
    tile = size // 2
    return pl.pallas_call(
        functools.partial(join_kernel, columns),
        grid=(2,),
        in_specs=[pl.BlockSpec((tile, piece.shape[1]), lambda i: (i, 0)) for piece in pieces],
        out_specs=pl.BlockSpec((tile, total), lambda i: (i, 0)),
        out_shape=jax.ShapeDtypeStruct((size, total), jnp.float32),
        cost_estimate=pl.CostEstimate(flops=0, bytes_accessed=8 * size * total, transcendentals=0),
        compiler_params=pltpu.CompilerParams(vmem_limit_bytes=16 * MIB),
        name="join",
    )(*pieces)


def slots_of(destination, owners, capacity):
    onehot = destination[:, None] == jnp.arange(owners, dtype=jnp.int32)[None, :]
    onehot = onehot.astype(jnp.float32).reshape(-1, 128, owners)
    lower = jnp.tril(jnp.ones((128, 128), jnp.float32), -1)
    within = jnp.einsum("rs,bso->bro", lower, onehot)
    sums = jnp.sum(onehot, axis=1)
    ahead = jnp.cumsum(sums, axis=0) - sums
    rank = jnp.sum((within + ahead[:, None, :]) * onehot, axis=2)
    return destination * capacity + rank.reshape(-1).astype(jnp.int32)


def local(pivot_rows, sections, sect_vectors, sect_factors, routes, parent_vectors, parent_factor):
    me = lax.axis_index("sect")
    count = lax.axis_size("sect")
    owners = lax.axis_size("front")
    pivots = in_hbm(pivot_rows[0, 0])
    sections, sect_vectors = in_hbm(sections[0, 0]), in_hbm(sect_vectors[0, 0])
    sect_factors = in_hbm(sect_factors[0, 0])
    panels, rows = sections.shape[:2]
    capacity = 3 * panels * rows // (2 * owners)
    total = owners * capacity
    panel_at = [((me - step) % count).astype(jnp.int32)[None] for step in range(count)]
    slots = slots_of(routes[0, 0, :, 0], owners, capacity)
    bases = jnp.concatenate(panel_at) * rows
    owner = me.astype(jnp.int32)[None]
    vectors, factor = parent_vectors[0, 0], parent_factor[0]
    weights = stage(jnp.concatenate(panel_at[1:]), sect_vectors, sect_factors)
    tops, out = [], None
    for streams in CHUNKS:
        column, width = streams[0][0], sum(width for _, width in streams)
        updated, moving = [], []
        for first, narrow in streams:
            pivot, blocks = pivots, []
            for step in range(count - 1):
                direct = step == 0
                pivot, block = reflect(
                    panel_at[step], step, pivot, first, narrow, sections,
                    (sect_vectors, sect_factors) if direct else weights,
                )
                blocks.append(block)
                pivot = passed_along(pivot, 1)
            updated.append(blocks)
            moving.append(pivot)
        packed = pack(bases, slots, updated, total)
        others = []
        for stream, (first, narrow) in enumerate(streams):
            last = stream == len(streams) - 1
            if last:
                pivot, packed = reflect_last(
                    panel_at[-1], count - 1, slots, moving[stream], first, sections, weights,
                    packed, others,
                )
            else:
                pivot, block = reflect(
                    panel_at[-1], count - 1, moving[stream], first, narrow, sections, weights
                )
                others.append(block)
            tops.append(passed_along(pivot, 1))
        arrived = lax.all_to_all(
            packed.reshape(owners, capacity, width), "front", split_axis=0, concat_axis=0, tiled=True
        ).reshape(total, width)
        own, *others = project(owner, vectors, arrived, count)
        others = [passed_along(part, away + 1) for away, part in enumerate(others)]
        for part in others:
            own = own + part
        parts = [own] + [passed_along(own, away) for away in range(1, count)]
        out = finish(owner, factor, vectors, arrived, parts, out, column // width, sections.shape[-1])
    top = join([column for streams in CHUNKS for column, _ in streams], tops)
    return (top[None, None], out[None, None])


def in_hbm(value):
    return pltpu.with_memory_space_constraint(value, pltpu.HBM)


def solution(mesh):
    in_specs = (
        P("front", "sect", None, None),
        P("front", "sect", None, None, None),
        P("front", "sect", None, None, None),
        P("front", "sect", None, None, None),
        P("front", "sect", None, None),
        P("front", "sect", None, None),
        P("front", None, None),
    )
    out_specs = (P("front", "sect", None, None), P("front", "sect", None, None))
    return jax.shard_map(local, mesh=mesh, in_specs=in_specs, out_specs=out_specs, check_vma=False)
```
